32 devices in a mesh: dp: 8 (over z, y), tensor: 4 (over x, core).
Axes of the slice: x: 2, y: 2, z: 4, core: 2. Of those that a mesh axis runs over, the one named last changes fastest.
Arguments:
- hidden_states: bfloat16 [16, 320, 1024], P('dp', None, 'tensor'), may hold values from -6 to 6
- output_grad: bfloat16 [16, 320, 1024], P('dp', None, 'tensor'), may hold values from -6 to 6
- group_counts: int32 [8], P('dp'), may hold values from 1 to 2, as said below
- gain_attention: float32 [1024], replicated, may hold values from 0.5 to 1.5
- shift_attention: float32 [1024], replicated, may hold values from -3 to 3
- gain_feedforward: float32 [1024], replicated, may hold values from 0.5 to 1.5
- shift_feedforward: float32 [1024], replicated, may hold values from -3 to 3
- heads_weight: bfloat16 [1024, 3, 1024], P(None, None, 'tensor'), may hold values from -0.1875 to 0.1875
- heads_bias: float32 [3, 1024], P(None, 'tensor'), may hold values from -3 to 3
- merge_weight: bfloat16 [1024, 1024], P('tensor'), may hold values from -0.75 to 0.75
- merge_bias: float32 [1024], P('tensor'), may hold values from -3 to 3
- expand_weight: bfloat16 [1024, 4096], P(None, 'tensor'), may hold values from -0.1875 to 0.1875
- expand_bias: float32 [4096], P('tensor'), may hold values from -3 to 3
- contract_weight: bfloat16 [4096, 1024], P('tensor'), may hold values from -0.09375 to 0.09375
- contract_bias: float32 [1024], P('tensor'), may hold values from -3 to 3
Outputs:
- block_output: bfloat16 [16, 320, 1024], P('dp', None, 'tensor')
- input_grad: bfloat16 [16, 320, 1024], P('dp', None, 'tensor')
- grad_gain_attention: float32 [1024], P('tensor')
- grad_shift_attention: float32 [1024], P('tensor')
- grad_gain_feedforward: float32 [1024], P('tensor')
- grad_shift_feedforward: float32 [1024], P('tensor')
- grad_heads_weight: float32 [1024, 3, 1024], P('dp', None, 'tensor')
- grad_heads_bias: float32 [3, 1024], P(None, 'tensor')
- grad_merge_weight: float32 [1024, 1024], P('tensor', 'dp')
- grad_merge_bias: float32 [1024], P('tensor')
- grad_expand_weight: float32 [1024, 4096], P('dp', 'tensor')
- grad_expand_bias: float32 [4096], P('tensor')
- grad_contract_weight: float32 [4096, 1024], P('tensor', 'dp')
- grad_contract_bias: float32 [1024], P('tensor')
The draws below stay inside these ranges and needn't reach their ends.
Inputs may be any that keep to these rules, and one draw needn't show every extreme that they name: `group_counts`: each index of dp has 1 or 2 live sequences in its first slots; slots after them are padding, and at least one index has 2.
All inputs are finite; a program needn't handle non-finite values.
Results may differ from the reference program's by a relative error of at most 0.015.
Values may be sent and summed in bfloat16 or wider, within the bound.
A program may use at most 128 MiB of HBM per device.

```python
import math
import jax
import jax.numpy as jnp
from jax import lax

D = 1024
HEADS = 16
HEAD_DIM = 64
FF = 4096
ROT = 16
LENGTH = 320
SLOTS = 2
SEQS = 16
N_DP = 8


def draw_group_counts(key, part):
    doubled = max(1, N_DP * 19 // 64)
    order = jax.random.permutation(key, N_DP)
    return jnp.where(order < doubled, SLOTS, 1).astype(jnp.int32)


def with_spikes(array, key, source, target, parts, factor):
    def block_of(dim):
        return (jnp.arange(array.shape[dim]) // (array.shape[dim] // parts)).reshape((-1,) + (1,) * (array.ndim - 1 - dim))

    one_side = jax.random.permutation(key, parts)[block_of(target)]
    second = (block_of(target) + parts // 2) % parts
    return jnp.where((block_of(source) == one_side) | (block_of(source) == second), factor * array, array)


def block_levels(own_key, dims, cuts, smallest, top_value):
    factor_of = 1.0
    for axis_at, shards_of in cuts:
        steps = jax.random.uniform(jax.random.fold_in(jax.random.fold_in(own_key, 6), axis_at), (shards_of,), jnp.float32, smallest / len(cuts), top_value / len(cuts))
        factor_of = factor_of * jnp.repeat(jnp.exp(steps), dims[axis_at] // shards_of).reshape((-1,) + (1,) * (len(dims) - 1 - axis_at))
    return factor_of


def normal_values(key, dims, spread, bound, cuts=(), kind=jnp.bfloat16):
    drawn = jax.random.normal(key, dims, jnp.float32) * spread
    if len(cuts) > 0:
        drawn = block_levels(key, dims, cuts, -0.22, 0.18) * drawn
    return jnp.clip(drawn, min=-bound, max=bound).astype(kind)


def heavy_noise(stream_key, shape, scale, limit, cuts, heavy, held_as=jnp.bfloat16):
    entries = scale * jax.random.normal(stream_key, shape, jnp.float32)
    if cuts:
        entries = entries * block_levels(stream_key, shape, cuts, -0.22, 0.18)
    return jnp.clip(with_spikes(entries, jax.random.fold_in(stream_key, 3), *heavy), -limit, limit).astype(held_as)


def setup_inputs(seed: int = 0) -> dict:
    splits = jax.random.split(jax.random.key(seed), 16)
    return {
        "hidden_states": heavy_noise(splits[0], (SEQS, LENGTH, D), 1.0, 6.0, ((0, 8), (2, 4)), (0, 2, 8, 2.0)),
        "output_grad": heavy_noise(splits[1], (SEQS, LENGTH, D), 1.0, 6.0, ((0, 8), (2, 4)), (0, 2, 8, 2.0)),
        "group_counts": draw_group_counts(jax.random.fold_in(splits[15], 71), 0),
        "gain_attention": jnp.clip(1.0 + 0.1 * jax.random.normal(splits[3], (D,), jnp.float32), 0.5, 1.5),
        "shift_attention": normal_values(splits[4], (D,), 0.5, 3.0, (), jnp.float32),
        "gain_feedforward": jnp.clip(1.0 + 0.1 * jax.random.normal(splits[5], (D,), jnp.float32), 0.5, 1.5),
        "shift_feedforward": normal_values(splits[6], (D,), 0.5, 3.0, (), jnp.float32),
        "heads_weight": normal_values(splits[7], (D, 3, D), D ** -0.5, 0.1875, ((2, 4),)),
        "heads_bias": normal_values(splits[8], (3, D), 0.5, 3.0, ((1, 4),), jnp.float32),
        "merge_weight": normal_values(splits[9], (D, D), HEAD_DIM ** -0.5, 0.75, ((0, 4),)),
        "merge_bias": normal_values(splits[10], (D,), 0.5, 3.0, ((0, 4),), jnp.float32),
        "expand_weight": normal_values(splits[11], (D, FF), D ** -0.5, 0.1875, ((1, 4),)),
        "expand_bias": normal_values(splits[12], (FF,), 0.5, 3.0, ((0, 4),), jnp.float32),
        "contract_weight": normal_values(splits[13], (FF, D), FF ** -0.5, 0.09375, ((0, 4),)),
        "contract_bias": normal_values(splits[14], (D,), 0.5, 3.0, ((0, 4),), jnp.float32),
    }


EPSILON = 1e-05

def settle(values):
    return lax.optimization_barrier(values.astype(jnp.bfloat16))

def rotary_tables(length):
    half_rot = ROT // 2
    position = jnp.arange(length, dtype=jnp.float32)[:, None]
    exponent = jnp.arange(half_rot, dtype=jnp.float32) * (2.0 / ROT)
    angles = position * jnp.exp(-math.log(10000.0) * exponent)[None, :]
    return (jnp.cos(angles), jnp.sin(angles))

def rotate_heads(values, cosine_table, sine_table, direction):
    half_rot = ROT // 2
    leading = values[..., :half_rot]
    trailing = values[..., half_rot:ROT]
    remainder = values[..., ROT:]
    turned = sine_table * direction
    return jnp.concatenate([leading * cosine_table - trailing * turned, trailing * cosine_table + leading * turned, remainder], axis=-1)

def gelu_value(hidden):
    return 0.5 * hidden * (1.0 + lax.erf(hidden * 0.7071067811865476))

def gelu_slope(hidden):
    return 0.5 * (1.0 + lax.erf(hidden * 0.7071067811865476)) + hidden * jnp.exp(-0.5 * hidden * hidden) * 0.3989422804014327

def norm_forward(values, gain, offset):
    center = lax.optimization_barrier(jnp.mean(values, axis=-1, keepdims=True))
    shifted = values - center
    inverse = lax.rsqrt(lax.optimization_barrier(jnp.mean(shifted * shifted, axis=-1, keepdims=True)) + EPSILON)
    normed = shifted * inverse
    return (normed, inverse, normed * gain + offset)

def norm_backward(upstream, normed, inverse, gain):
    scaled = upstream * gain
    return inverse * (scaled - lax.optimization_barrier(jnp.mean(scaled, axis=-1, keepdims=True)) - normed * lax.optimization_barrier(jnp.mean(scaled * normed, axis=-1, keepdims=True)))

def causal_scores(query, keys):
    scores = jnp.einsum('bhqd,bhkd->bhqk', query.astype(jnp.float32), keys.astype(jnp.float32))
    length = scores.shape[-1]
    allowed = jnp.arange(length, dtype=jnp.int32)[:, None] >= jnp.arange(length, dtype=jnp.int32)[None, :]
    return jnp.where(allowed, scores, -1e+30)

def reference(hidden_states, output_grad, group_counts, gain_attention, shift_attention, gain_feedforward, shift_feedforward, heads_weight, heads_bias, merge_weight, merge_bias, expand_weight, expand_bias, contract_weight, contract_bias):
    slot_index = jnp.arange(SEQS, dtype=jnp.int32)
    live_slots = (slot_index % SLOTS < group_counts[slot_index // SLOTS]).astype(jnp.float32)
    per_block = math.gcd(SEQS, max(1, 4096 // LENGTH))
    block_count = SEQS // per_block
    head_scale = 1.0 / math.sqrt(HEAD_DIM)
    cosine_table, sine_table = rotary_tables(LENGTH)
    flat_heads = heads_weight.reshape(D, 3 * D)
    rows = per_block * LENGTH

    def one_block(totals, pieces):
        tokens, upstream, live = pieces
        residual = tokens.astype(jnp.float32).reshape(rows, D)
        normed_one, inverse_one, attn_norm = norm_forward(residual, gain_attention, shift_attention)
        normed_two, inverse_two, ffn_norm = norm_forward(residual, gain_feedforward, shift_feedforward)
        attn_input = settle(attn_norm)
        ffn_input = settle(ffn_norm)
        projected = jnp.dot(attn_input, flat_heads, preferred_element_type=jnp.float32).reshape(per_block, LENGTH, 3, HEADS, HEAD_DIM) + heads_bias.reshape(3, HEADS, HEAD_DIM)
        query = settle(rotate_heads(jnp.transpose(projected[:, :, 0], (0, 2, 1, 3)), cosine_table, sine_table, 1.0) * head_scale)
        keys = settle(rotate_heads(jnp.transpose(projected[:, :, 1], (0, 2, 1, 3)), cosine_table, sine_table, 1.0))
        values = settle(jnp.transpose(projected[:, :, 2], (0, 2, 1, 3)))
        scores = causal_scores(query, keys)
        row_peak = lax.optimization_barrier(jnp.max(scores, axis=-1, keepdims=True))
        logsum = row_peak + jnp.log(lax.optimization_barrier(jnp.sum(jnp.exp(scores - row_peak), axis=-1, keepdims=True)))
        probs = settle(jnp.exp(scores - logsum))
        context = settle(jnp.einsum('bhqk,bhkd->bhqd', probs.astype(jnp.float32), values.astype(jnp.float32)))
        context_rows = jnp.transpose(context, (0, 2, 1, 3)).reshape(rows, D)
        attn_part = jnp.dot(context_rows, merge_weight, preferred_element_type=jnp.float32)
        pre_active = jnp.dot(ffn_input, expand_weight, preferred_element_type=jnp.float32) + expand_bias
        active = settle(gelu_value(pre_active))
        ffn_part = jnp.dot(active, contract_weight, preferred_element_type=jnp.float32)
        block_output = (residual + (attn_part + ffn_part) + merge_bias + contract_bias).astype(jnp.bfloat16)
        masked = settle(upstream.astype(jnp.float32) * live[:, None, None]).reshape(rows, D)
        masked_full = masked.astype(jnp.float32)
        grad_out_bias = lax.optimization_barrier(jnp.sum(masked_full, axis=0))
        grad_merge = jnp.dot(context_rows.T, masked, preferred_element_type=jnp.float32)
        grad_contract = jnp.dot(active.T, masked, preferred_element_type=jnp.float32)
        active_grad = jnp.dot(masked, contract_weight.T, preferred_element_type=jnp.float32) * gelu_slope(pre_active)
        grad_expand_bias = lax.optimization_barrier(jnp.sum(active_grad, axis=0))
        active_grad16 = settle(active_grad)
        grad_expand = jnp.dot(ffn_input.T, active_grad16, preferred_element_type=jnp.float32)
        ffn_back = jnp.dot(active_grad16, expand_weight.T, preferred_element_type=jnp.float32)
        context_grad = settle(jnp.dot(masked, merge_weight.T, preferred_element_type=jnp.float32))
        context_grad = jnp.transpose(context_grad.reshape(per_block, LENGTH, HEADS, HEAD_DIM), (0, 2, 1, 3))
        probs_again = jnp.exp(scores - logsum)
        prob_grad = jnp.einsum('bhqd,bhkd->bhqk', context_grad.astype(jnp.float32), values.astype(jnp.float32))
        delta = lax.optimization_barrier(jnp.sum(context_grad.astype(jnp.float32) * context.astype(jnp.float32), axis=-1, keepdims=True))
        score_grad = settle(probs_again * (prob_grad - delta))
        query_grad = jnp.einsum('bhqk,bhkd->bhqd', score_grad.astype(jnp.float32), keys.astype(jnp.float32)) * head_scale
        keys_grad = jnp.einsum('bhqk,bhqd->bhkd', score_grad.astype(jnp.float32), query.astype(jnp.float32))
        values_grad = jnp.einsum('bhqk,bhqd->bhkd', probs.astype(jnp.float32), context_grad.astype(jnp.float32))
        query_grad = rotate_heads(query_grad, cosine_table, sine_table, -1.0)
        keys_grad = rotate_heads(keys_grad, cosine_table, sine_table, -1.0)
        heads_grad = jnp.transpose(jnp.stack([query_grad, keys_grad, values_grad], axis=1), (0, 3, 1, 2, 4)).reshape(rows, 3 * D)
        grad_heads_bias = lax.optimization_barrier(jnp.sum(heads_grad, axis=0)).reshape(3, D)
        heads_grad16 = settle(heads_grad)
        grad_heads = jnp.dot(attn_input.T, heads_grad16, preferred_element_type=jnp.float32).reshape(D, 3, D)
        attn_back = jnp.dot(heads_grad16, flat_heads.T, preferred_element_type=jnp.float32)
        input_grad = (masked_full + norm_backward(attn_back, normed_one, inverse_one, gain_attention) + norm_backward(ffn_back, normed_two, inverse_two, gain_feedforward)).astype(jnp.bfloat16)
        update = (lax.optimization_barrier(jnp.sum(attn_back * normed_one, axis=0)), lax.optimization_barrier(jnp.sum(attn_back, axis=0)), lax.optimization_barrier(jnp.sum(ffn_back * normed_two, axis=0)), lax.optimization_barrier(jnp.sum(ffn_back, axis=0)), grad_heads, grad_heads_bias, grad_merge, grad_out_bias, grad_expand, grad_expand_bias, grad_contract)
        totals = jax.tree.map(jnp.add, totals, update)
        return (totals, (block_output.reshape(per_block, LENGTH, D), input_grad.reshape(per_block, LENGTH, D)))
    initial = (jnp.zeros((D,), jnp.float32), jnp.zeros((D,), jnp.float32), jnp.zeros((D,), jnp.float32), jnp.zeros((D,), jnp.float32), jnp.zeros((D, 3, D), jnp.float32), jnp.zeros((3, D), jnp.float32), jnp.zeros((D, D), jnp.float32), jnp.zeros((D,), jnp.float32), jnp.zeros((D, FF), jnp.float32), jnp.zeros((FF,), jnp.float32), jnp.zeros((FF, D), jnp.float32))
    stacked = (hidden_states.reshape(block_count, per_block, LENGTH, D), output_grad.reshape(block_count, per_block, LENGTH, D), live_slots.reshape(block_count, per_block))
    totals, (outputs, grads) = lax.scan(one_block, initial, stacked)
    return (outputs.reshape(SEQS, LENGTH, D), grads.reshape(SEQS, LENGTH, D), totals[0], totals[1], totals[2], totals[3], totals[4], totals[5], totals[6], totals[7], totals[8], totals[9], totals[10], totals[7])
```

```python
import math

import jax
import jax.numpy as jnp
from jax import lax
from jax.sharding import PartitionSpec as P

HEAD_DIM = 64
ROT = 16


EPSILON = 1e-05


def rotary_tables(length):
    half_rot = ROT // 2
    position = jnp.arange(length, dtype=jnp.float32)[:, None]
    exponent = jnp.arange(half_rot, dtype=jnp.float32) * (2.0 / ROT)
    angles = position * jnp.exp(-math.log(10000.0) * exponent)[None, :]
    return (jnp.cos(angles), jnp.sin(angles))


def rotate_heads(values, cosine_table, sine_table, direction):
    half_rot = ROT // 2
    leading = values[..., :half_rot]
    trailing = values[..., half_rot:ROT]
    remainder = values[..., ROT:]
    turned = sine_table * direction
    return jnp.concatenate(
        [
            leading * cosine_table - trailing * turned,
            trailing * cosine_table + leading * turned,
            remainder,
        ],
        axis=-1,
    )


def gelu_value(hidden):
    return 0.5 * hidden * (1.0 + lax.erf(hidden * 0.7071067811865476))


def gelu_slope(hidden):
    return (
        0.5 * (1.0 + lax.erf(hidden * 0.7071067811865476))
        + hidden * jnp.exp(-0.5 * hidden * hidden) * 0.3989422804014327
    )


def norm_forward(values, gain, offset):
    center = jnp.mean(values, axis=-1, keepdims=True)
    shifted = values - center
    inverse = lax.rsqrt(jnp.mean(shifted * shifted, axis=-1, keepdims=True) + EPSILON)
    normed = shifted * inverse
    return (normed, inverse, normed * gain + offset)


def causal_scores(query, keys):
    scores = jnp.einsum("bhqd,bhkd->bhqk", query, keys, preferred_element_type=jnp.float32)
    length = scores.shape[-1]
    allowed = jnp.arange(length)[:, None] >= jnp.arange(length)[None, :]
    return jnp.where(allowed, scores, -1e30)


def own_columns(array, start, count):
    return lax.dynamic_slice_in_dim(array, start, count, axis=array.ndim - 1)


def body(
    hidden_states,
    output_grad,
    group_counts,
    gain_attention,
    shift_attention,
    gain_feedforward,
    shift_feedforward,
    heads_weight,
    heads_bias,
    merge_weight,
    merge_bias,
    expand_weight,
    expand_bias,
    contract_weight,
    contract_bias,
):
    slots, length, local_width = hidden_states.shape
    width = gain_attention.shape[0]
    rows = slots * length
    local_heads = local_width // HEAD_DIM
    head_scale = 1.0 / math.sqrt(HEAD_DIM)
    start = lax.axis_index("tensor") * local_width
    full_states, full_grad = (
        lax.all_gather(hidden_states, "tensor", axis=2, tiled=True),
        lax.all_gather(output_grad, "tensor", axis=2, tiled=True),
    )
    live = (jnp.arange(slots) < group_counts[0]).astype(jnp.float32)
    cosine_table, sine_table = rotary_tables(length)
    residual = full_states.astype(jnp.float32).reshape(rows, width)
    normed_one, inverse_one, attn_norm = norm_forward(residual, gain_attention, shift_attention)
    ffn_norm = normed_one * gain_feedforward + shift_feedforward
    attn_input = attn_norm.astype(jnp.bfloat16)
    ffn_input = ffn_norm.astype(jnp.bfloat16)
    flat_heads = heads_weight.reshape(width, 3 * local_width)
    projected = jnp.dot(attn_input, flat_heads, preferred_element_type=jnp.float32).reshape(
        slots, length, 3, local_heads, HEAD_DIM
    ) + heads_bias.reshape(3, local_heads, HEAD_DIM)
    query = (
        rotate_heads(jnp.transpose(projected[:, :, 0], (0, 2, 1, 3)), cosine_table, sine_table, 1.0)
        * head_scale
    ).astype(jnp.bfloat16)
    keys = rotate_heads(
        jnp.transpose(projected[:, :, 1], (0, 2, 1, 3)), cosine_table, sine_table, 1.0
    ).astype(jnp.bfloat16)
    values = jnp.transpose(projected[:, :, 2], (0, 2, 1, 3)).astype(jnp.bfloat16)
    scores = causal_scores(query, keys)
    row_peak = jnp.max(scores, axis=-1, keepdims=True)
    logsum = row_peak + jnp.log(jnp.sum(jnp.exp(scores - row_peak), axis=-1, keepdims=True))
    probs = jnp.exp(scores - logsum).astype(jnp.bfloat16)
    context = jnp.einsum(
        "bhqk,bhkd->bhqd", probs, values, preferred_element_type=jnp.float32
    ).astype(jnp.bfloat16)
    context_rows = jnp.transpose(context, (0, 2, 1, 3)).reshape(rows, local_width)
    attn_part = jnp.dot(context_rows, merge_weight, preferred_element_type=jnp.float32)
    pre_active = jnp.dot(ffn_input, expand_weight, preferred_element_type=jnp.float32) + expand_bias
    active = gelu_value(pre_active).astype(jnp.bfloat16)
    ffn_part = jnp.dot(active, contract_weight, preferred_element_type=jnp.float32)
    summed = lax.psum_scatter(
        (attn_part + ffn_part).astype(jnp.bfloat16).reshape(slots, length, width),
        "tensor",
        scatter_dimension=2,
        tiled=True,
    ).astype(jnp.float32)
    block_output = (hidden_states.astype(jnp.float32) + summed + merge_bias + contract_bias).astype(
        jnp.bfloat16
    )
    masked = (
        (full_grad.astype(jnp.float32) * live[:, None, None])
        .astype(jnp.bfloat16)
        .reshape(rows, width)
    )
    own_masked = (output_grad.astype(jnp.float32) * live[:, None, None]).reshape(rows, local_width)
    grad_out_bias = jnp.sum(own_masked, axis=0)
    grad_merge = jnp.dot(context_rows.T, masked, preferred_element_type=jnp.float32)
    grad_contract = jnp.dot(active.T, masked, preferred_element_type=jnp.float32)
    active_grad = jnp.dot(
        masked, contract_weight.T, preferred_element_type=jnp.float32
    ) * gelu_slope(pre_active)
    grad_expand_bias = jnp.sum(active_grad, axis=0)
    active_grad16 = active_grad.astype(jnp.bfloat16)
    grad_expand = jnp.dot(ffn_input.T, active_grad16, preferred_element_type=jnp.float32)
    ffn_back = jnp.dot(active_grad16, expand_weight.T, preferred_element_type=jnp.float32)
    context_grad = jnp.dot(masked, merge_weight.T, preferred_element_type=jnp.float32).astype(
        jnp.bfloat16
    )
    context_grad = jnp.transpose(
        context_grad.reshape(slots, length, local_heads, HEAD_DIM), (0, 2, 1, 3)
    )
    probs_again = jnp.exp(causal_scores(query, keys) - logsum)
    prob_grad = jnp.einsum(
        "bhqd,bhkd->bhqk", context_grad, values, preferred_element_type=jnp.float32
    )
    delta = jnp.sum(
        context_grad.astype(jnp.float32) * context.astype(jnp.float32), axis=-1, keepdims=True
    )
    score_grad = (probs_again * (prob_grad - delta)).astype(jnp.bfloat16)
    query_grad = (
        jnp.einsum("bhqk,bhkd->bhqd", score_grad, keys, preferred_element_type=jnp.float32)
        * head_scale
    )
    keys_grad = jnp.einsum("bhqk,bhqd->bhkd", score_grad, query, preferred_element_type=jnp.float32)
    values_grad = jnp.einsum(
        "bhqk,bhqd->bhkd", probs, context_grad, preferred_element_type=jnp.float32
    )
    query_grad = rotate_heads(query_grad, cosine_table, sine_table, -1.0)
    keys_grad = rotate_heads(keys_grad, cosine_table, sine_table, -1.0)
    heads_grad = jnp.transpose(
        jnp.stack([query_grad, keys_grad, values_grad], axis=1), (0, 3, 1, 2, 4)
    ).reshape(rows, 3 * local_width)
    grad_heads_bias = jnp.sum(heads_grad, axis=0).reshape(3, local_width)
    heads_grad16 = heads_grad.astype(jnp.bfloat16)
    grad_heads = jnp.dot(attn_input.T, heads_grad16, preferred_element_type=jnp.float32).reshape(
        width, 3, local_width
    )
    attn_back = jnp.dot(heads_grad16, flat_heads.T, preferred_element_type=jnp.float32)
    sent_contract, sent_expand, sent_merge, sent_heads = (
        lax.psum_scatter(
            grad_contract.astype(jnp.bfloat16), "dp", scatter_dimension=1, tiled=True
        ).astype(jnp.float32),
        lax.psum_scatter(
            grad_expand.astype(jnp.bfloat16), "dp", scatter_dimension=0, tiled=True
        ).astype(jnp.float32),
        lax.psum_scatter(
            grad_merge.astype(jnp.bfloat16), "dp", scatter_dimension=1, tiled=True
        ).astype(jnp.float32),
        lax.psum_scatter(
            grad_heads.astype(jnp.bfloat16), "dp", scatter_dimension=0, tiled=True
        ).astype(jnp.float32),
    )
    scaled = attn_back * gain_attention + ffn_back * gain_feedforward
    stats = lax.psum(
        jnp.stack([jnp.sum(scaled, axis=-1), jnp.sum(scaled * normed_one, axis=-1)]), "tensor"
    )
    scaled_own = lax.psum_scatter(
        scaled.astype(jnp.bfloat16), "tensor", scatter_dimension=1, tiled=True
    ).astype(jnp.float32)
    normed_own = own_columns(normed_one, start, local_width)
    input_grad = own_masked + inverse_one * (
        scaled_own - stats[0][:, None] / width - normed_own * (stats[1][:, None] / width)
    )
    norm_sums = lax.psum(
        jnp.stack(
            [
                jnp.sum(attn_back * normed_one, axis=0),
                jnp.sum(attn_back, axis=0),
                jnp.sum(ffn_back * normed_one, axis=0),
                jnp.sum(ffn_back, axis=0),
            ]
        ),
        ("dp", "tensor"),
    )
    norm_own = own_columns(norm_sums, start, local_width)
    sums = lax.psum(
        jnp.concatenate([grad_out_bias, grad_heads_bias.reshape(-1), grad_expand_bias]), "dp"
    )
    vectors = (
        norm_own[0],
        norm_own[1],
        norm_own[2],
        norm_own[3],
        sums[:local_width],
        sums[local_width : 4 * local_width].reshape(3, local_width),
        sums[4 * local_width :],
    )
    input_grad = input_grad.astype(jnp.bfloat16).reshape(slots, length, local_width)
    return (
        block_output,
        input_grad,
        vectors[0],
        vectors[1],
        vectors[2],
        vectors[3],
        sent_heads,
        vectors[5],
        sent_merge,
        vectors[4],
        sent_expand,
        vectors[6],
        sent_contract,
        vectors[4],
    )


def solution(mesh):
    placed = (
        P("dp", None, "tensor"),
        P("dp", None, "tensor"),
        P("dp"),
        P(),
        P(),
        P(),
        P(),
        P(None, None, "tensor"),
        P(None, "tensor"),
        P("tensor", None),
        P("tensor"),
        P(None, "tensor"),
        P("tensor"),
        P("tensor", None),
        P("tensor"),
    )
    return jax.shard_map(
        body,
        mesh=mesh,
        in_specs=placed,
        out_specs=(
            P("dp", None, "tensor"),
            P("dp", None, "tensor"),
            P("tensor"),
            P("tensor"),
            P("tensor"),
            P("tensor"),
            P("dp", None, "tensor"),
            P(None, "tensor"),
            P("tensor", "dp"),
            P("tensor"),
            P("dp", "tensor"),
            P("tensor"),
            P("tensor", "dp"),
            P("tensor"),
        ),
        check_vma=False,
    )
```

```python
import math

import jax
import jax.numpy as jnp
from jax import lax
from jax.sharding import PartitionSpec as P

HEAD_DIM = 64
ROT = 16


EPSILON = 1e-05


def rotary_tables(length):
    half_rot = ROT // 2
    position = jnp.arange(length, dtype=jnp.float32)[:, None]
    exponent = jnp.arange(half_rot, dtype=jnp.float32) * (2.0 / ROT)
    angles = position * jnp.exp(-math.log(10000.0) * exponent)[None, :]
    return (jnp.cos(angles), jnp.sin(angles))


def rotate_heads(values, cosine_table, sine_table, direction):
    half_rot = ROT // 2
    leading = values[..., :half_rot]
    trailing = values[..., half_rot:ROT]
    remainder = values[..., ROT:]
    turned = sine_table * direction
    return jnp.concatenate(
        [
            leading * cosine_table - trailing * turned,
            trailing * cosine_table + leading * turned,
            remainder,
        ],
        axis=-1,
    )


def gelu_value(hidden):
    return 0.5 * hidden * (1.0 + lax.erf(hidden * 0.7071067811865476))


def gelu_slope(hidden):
    return (
        0.5 * (1.0 + lax.erf(hidden * 0.7071067811865476))
        + hidden * jnp.exp(-0.5 * hidden * hidden) * 0.3989422804014327
    )


def norm_forward(values, gain, offset):
    center = jnp.mean(values, axis=-1, keepdims=True)
    shifted = values - center
    inverse = lax.rsqrt(jnp.mean(shifted * shifted, axis=-1, keepdims=True) + EPSILON)
    normed = shifted * inverse
    return (normed, inverse, normed * gain + offset)


def causal_scores(query, keys):
    scores = jnp.einsum("bhqd,bhkd->bhqk", query, keys, preferred_element_type=jnp.float32)
    length = scores.shape[-1]
    allowed = jnp.arange(length)[:, None] >= jnp.arange(length)[None, :]
    return jnp.where(allowed, scores, -1e30)


def hop(array, axis, bit):
    size = lax.axis_size(axis)
    return lax.ppermute(array, axis, [(i, i ^ bit) for i in range(size)])


def relative_blocks(array, axis_name, order, axis):
    count = lax.axis_size(axis_name)
    size = array.shape[axis] // count
    me = lax.axis_index(axis_name)
    levels = len(order)
    pieces = []
    for r in range(count):
        mask = sum(bit for k, bit in enumerate(order) if (r >> (levels - 1 - k)) & 1)
        pieces.append(lax.dynamic_slice_in_dim(array, (me ^ mask) * size, size, axis=axis))
    return jnp.concatenate(pieces, axis=axis)


def halves(array, axis):
    count = array.shape[axis] // 2
    return (
        lax.slice_in_dim(array, 0, count, axis=axis),
        lax.slice_in_dim(array, count, 2 * count, axis=axis),
    )


def scatter_halves(kept, sent, axis_name, order, axis, wire):
    for step, bit in enumerate(order):
        if step:
            kept, sent = halves(kept, axis)
        kept = kept + hop(sent.astype(wire), axis_name, bit).astype(jnp.float32)
    return kept


def transposed_dot(left, right):
    return lax.dot_general(
        left, right, (((0,), (0,)), ((), ())), preferred_element_type=jnp.float32
    )


def scatter_products(whole, pair, order, axis):
    if axis:
        sent, kept = transposed_dot(whole, pair[1]), transposed_dot(whole, pair[0])
    else:
        sent, kept = transposed_dot(pair[1], whole), transposed_dot(pair[0], whole)
    return scatter_halves(kept, sent, "dp", order, axis, jnp.bfloat16)


def add_all(array, axis_name, order):
    for bit in order:
        array = array + hop(array, axis_name, bit)
    return array


def gather_relative(array, axis_name, order):
    held = {0: array}
    for bit in order:
        held.update({r ^ bit: hop(block, axis_name, bit) for r, block in list(held.items())})
    return [held[r] for r in range(lax.axis_size(axis_name))]


def gather_columns(array, axis_name, order):
    blocks = jnp.stack(gather_relative(array, axis_name, order))
    me = lax.axis_index(axis_name)
    return jnp.concatenate(
        [
            lax.dynamic_index_in_dim(blocks, me ^ j, 0, keepdims=False)
            for j in range(blocks.shape[0])
        ],
        axis=-1,
    )


def powers(axis_name):
    return [1 << k for k in range(lax.axis_size(axis_name).bit_length() - 1)]


def own_columns(array, start, count):
    return lax.dynamic_slice_in_dim(array, start, count, axis=array.ndim - 1)


def body(
    hidden_states,
    output_grad,
    group_counts,
    gain_attention,
    shift_attention,
    gain_feedforward,
    shift_feedforward,
    heads_weight,
    heads_bias,
    merge_weight,
    merge_bias,
    expand_weight,
    expand_bias,
    contract_weight,
    contract_bias,
):
    slots, length, local_width = hidden_states.shape
    width = gain_attention.shape[0]
    rows = slots * length
    local_heads = local_width // HEAD_DIM
    head_scale = 1.0 / math.sqrt(HEAD_DIM)
    start = lax.axis_index("tensor") * local_width
    dp_order = powers("dp")
    dp_late = dp_order[1:] + dp_order[:1]
    tensor_order = powers("tensor")
    far_first = tensor_order[::-1]
    full_states = gather_columns(hidden_states, "tensor", far_first)
    full_grad = gather_columns(output_grad, "tensor", far_first)
    live = (jnp.arange(slots) < group_counts[0]).astype(jnp.float32)
    cosine_table, sine_table = rotary_tables(length)
    residual = full_states.astype(jnp.float32).reshape(rows, width)
    normed_one, inverse_one, attn_norm = norm_forward(residual, gain_attention, shift_attention)
    ffn_norm = normed_one * gain_feedforward + shift_feedforward
    attn_input = attn_norm.astype(jnp.bfloat16)
    ffn_input = ffn_norm.astype(jnp.bfloat16)
    flat_heads = heads_weight.reshape(width, 3 * local_width)
    projected = jnp.dot(attn_input, flat_heads, preferred_element_type=jnp.float32).reshape(
        slots, length, 3, local_heads, HEAD_DIM
    ) + heads_bias.reshape(3, local_heads, HEAD_DIM)
    query = (
        rotate_heads(jnp.transpose(projected[:, :, 0], (0, 2, 1, 3)), cosine_table, sine_table, 1.0)
        * head_scale
    ).astype(jnp.bfloat16)
    keys = rotate_heads(
        jnp.transpose(projected[:, :, 1], (0, 2, 1, 3)), cosine_table, sine_table, 1.0
    ).astype(jnp.bfloat16)
    values = jnp.transpose(projected[:, :, 2], (0, 2, 1, 3)).astype(jnp.bfloat16)
    scores = causal_scores(query, keys)
    row_peak = jnp.max(scores, axis=-1, keepdims=True)
    logsum = row_peak + jnp.log(jnp.sum(jnp.exp(scores - row_peak), axis=-1, keepdims=True))
    probs = jnp.exp(scores - logsum).astype(jnp.bfloat16)
    context = jnp.einsum(
        "bhqk,bhkd->bhqd", probs, values, preferred_element_type=jnp.float32
    ).astype(jnp.bfloat16)
    context_rows = jnp.transpose(context, (0, 2, 1, 3)).reshape(rows, local_width)
    attn_part = jnp.dot(context_rows, merge_weight, preferred_element_type=jnp.float32)
    pre_active = jnp.dot(ffn_input, expand_weight, preferred_element_type=jnp.float32) + expand_bias
    active = gelu_value(pre_active).astype(jnp.bfloat16)
    ffn_part = jnp.dot(active, contract_weight, preferred_element_type=jnp.float32)
    summed = scatter_halves(
        *halves(relative_blocks(attn_part + ffn_part, "tensor", tensor_order, 1), 1),
        "tensor",
        tensor_order,
        1,
        jnp.bfloat16,
    ).reshape(slots, length, local_width)
    block_output = (hidden_states.astype(jnp.float32) + summed + merge_bias + contract_bias).astype(
        jnp.bfloat16
    )
    masked = (
        (full_grad.astype(jnp.float32) * live[:, None, None])
        .astype(jnp.bfloat16)
        .reshape(rows, width)
    )
    own_masked = (output_grad.astype(jnp.float32) * live[:, None, None]).reshape(rows, local_width)
    grad_out_bias = jnp.sum(own_masked, axis=0)
    masked_halves = halves(relative_blocks(masked, "dp", dp_order, 1), 1)
    sent_contract = scatter_products(active, masked_halves, dp_order, 1)
    sent_merge = scatter_products(context_rows, masked_halves, dp_order, 1)
    active_grad = jnp.dot(
        masked, contract_weight.T, preferred_element_type=jnp.float32
    ) * gelu_slope(pre_active)
    grad_expand_bias = jnp.sum(active_grad, axis=0)
    active_grad16 = active_grad.astype(jnp.bfloat16)
    sent_expand = scatter_products(
        active_grad16, halves(relative_blocks(ffn_input, "dp", dp_order, 1), 1), dp_order, 0
    )
    ffn_back = jnp.dot(active_grad16, expand_weight.T, preferred_element_type=jnp.float32)
    context_grad = jnp.dot(masked, merge_weight.T, preferred_element_type=jnp.float32).astype(
        jnp.bfloat16
    )
    context_grad = jnp.transpose(
        context_grad.reshape(slots, length, local_heads, HEAD_DIM), (0, 2, 1, 3)
    )
    probs_again = jnp.exp(causal_scores(query, keys) - logsum)
    prob_grad = jnp.einsum(
        "bhqd,bhkd->bhqk", context_grad, values, preferred_element_type=jnp.float32
    )
    delta = jnp.sum(
        context_grad.astype(jnp.float32) * context.astype(jnp.float32), axis=-1, keepdims=True
    )
    score_grad = (probs_again * (prob_grad - delta)).astype(jnp.bfloat16)
    query_grad = (
        jnp.einsum("bhqk,bhkd->bhqd", score_grad, keys, preferred_element_type=jnp.float32)
        * head_scale
    )
    keys_grad = jnp.einsum("bhqk,bhqd->bhkd", score_grad, query, preferred_element_type=jnp.float32)
    values_grad = jnp.einsum(
        "bhqk,bhqd->bhkd", probs, context_grad, preferred_element_type=jnp.float32
    )
    query_grad = rotate_heads(query_grad, cosine_table, sine_table, -1.0)
    keys_grad = rotate_heads(keys_grad, cosine_table, sine_table, -1.0)
    heads_grad = jnp.transpose(
        jnp.stack([query_grad, keys_grad, values_grad], axis=1), (0, 3, 1, 2, 4)
    ).reshape(rows, 3 * local_width)
    grad_heads_bias = jnp.sum(heads_grad, axis=0).reshape(3, local_width)
    heads_grad16 = heads_grad.astype(jnp.bfloat16)
    sent_heads = scatter_products(
        heads_grad16, halves(relative_blocks(attn_input, "dp", dp_late, 1), 1), dp_late, 0
    ).reshape(-1, 3, local_width)
    attn_back = jnp.dot(heads_grad16, flat_heads.T, preferred_element_type=jnp.float32)
    scaled = attn_back * gain_attention + ffn_back * gain_feedforward
    stats = add_all(
        jnp.stack([jnp.sum(scaled, axis=-1), jnp.sum(scaled * normed_one, axis=-1)]),
        "tensor",
        tensor_order,
    )
    scaled_own = scatter_halves(
        *halves(relative_blocks(scaled, "tensor", tensor_order, 1), 1),
        "tensor",
        tensor_order,
        1,
        jnp.bfloat16,
    )
    normed_own = own_columns(normed_one, start, local_width)
    input_grad = own_masked + inverse_one * (
        scaled_own - stats[0][:, None] / width - normed_own * (stats[1][:, None] / width)
    )
    norm_sums = jnp.stack(
        [
            jnp.sum(attn_back * normed_one, axis=0),
            jnp.sum(attn_back, axis=0),
            jnp.sum(ffn_back * normed_one, axis=0),
            jnp.sum(ffn_back, axis=0),
        ]
    )
    norm_own = scatter_halves(
        *halves(relative_blocks(norm_sums, "tensor", tensor_order, 1), 1),
        "tensor",
        tensor_order,
        1,
        jnp.float32,
    )
    sums = add_all(
        jnp.concatenate(
            [
                grad_out_bias,
                grad_heads_bias.reshape(-1),
                grad_expand_bias,
                norm_own.reshape(-1),
            ]
        ),
        "dp",
        dp_order,
    )
    first = 4 * local_width
    second = first + grad_expand_bias.shape[0]
    norm_own = sums[second:].reshape(4, local_width)
    vectors = (
        norm_own[0],
        norm_own[1],
        norm_own[2],
        norm_own[3],
        sums[:local_width],
        sums[local_width:first].reshape(3, local_width),
        sums[first:second],
    )
    input_grad = input_grad.astype(jnp.bfloat16).reshape(slots, length, local_width)
    return (
        block_output,
        input_grad,
        vectors[0],
        vectors[1],
        vectors[2],
        vectors[3],
        sent_heads,
        vectors[5],
        sent_merge,
        vectors[4],
        sent_expand,
        vectors[6],
        sent_contract,
        vectors[4],
    )


def solution(mesh):
    placed = (
        P("dp", None, "tensor"),
        P("dp", None, "tensor"),
        P("dp"),
        P(),
        P(),
        P(),
        P(),
        P(None, None, "tensor"),
        P(None, "tensor"),
        P("tensor", None),
        P("tensor"),
        P(None, "tensor"),
        P("tensor"),
        P("tensor", None),
        P("tensor"),
    )
    return jax.shard_map(
        body,
        mesh=mesh,
        in_specs=placed,
        out_specs=(
            P("dp", None, "tensor"),
            P("dp", None, "tensor"),
            P("tensor"),
            P("tensor"),
            P("tensor"),
            P("tensor"),
            P("dp", None, "tensor"),
            P(None, "tensor"),
            P("tensor", "dp"),
            P("tensor"),
            P("dp", "tensor"),
            P("tensor"),
            P("tensor", "dp"),
            P("tensor"),
        ),
        check_vma=False,
    )
```
